128 devices in a mesh: row: 16 (over z, y_lo, core), col: 8 (over x, y_hi).
Axes of the slice: x: 4, y: 4 (y_hi: 2, y_lo: 2; y = y_hi * 2 + y_lo), z: 4, core: 2. Of those that a mesh axis runs over, the one named last changes fastest.
Arguments:
- hidden_acts: bfloat16 [16384, 29568], P('col', 'row'), may hold values from -6 to 6
- out_grads: bfloat16 [16384, 8192], P('col', 'row'), may hold values from -6 to 6
- proj_in: bfloat16 [29568, 64], P('row'), may hold values from -0.03125 to 0.03125
- proj_out: bfloat16 [8192, 64], P('row'), may hold values from -0.0625 to 0.0625
- white_in: float32 [64, 64], replicated, may hold values from -0.75 to 0.75
- white_out: float32 [64, 64], replicated, may hold values from -0.75 to 0.75
- ep_lengths: int32 [8, 64], P('col'), may hold values from 1 to 64, 2048 in all within a row
- flag_ids: int32 [64], replicated, may hold values from 0 to 511
- train_sketch: bfloat16 [131072, 4096], P('row', 'col'), may hold values from -0.01171875 to 0.01171875
Outputs:
- scores: float32 [64, 131072], P('col', 'row')
The draws below stay inside these ranges and needn't reach their ends.
Inputs may be any that keep to these rules, and one draw needn't show every extreme that they name: `ep_lengths`: each row holds 64 lengths summing to 2048, the largest exactly 64. `flag_ids`: indices may repeat.
All inputs are finite; a program needn't handle non-finite values.
Results may differ from the reference program's by a relative error of at most 0.0029.
Values may be sent and summed in bfloat16 or wider, within the bound.
A program may use at most 128 MiB of HBM per device.

```python
import math
import jax
import jax.numpy as jnp
import numpy as np
from jax import lax

D = 8192
FF = 29568
SK = 64
TOK_DEV = 2048
EP_DEV = 64
MOST = 64
TOKENS = 16384
EPISODES = 512
FLAGGED = 64
TRAIN = 131072
N_COL = 8


def place_ends(result, key, smallest, largest):
    extent = result.shape
    index_at = [jax.random.randint(jax.random.fold_in(key, axis), (), 0, extent[axis]) for axis in range(len(extent))]
    result = result.at[tuple(index_at)].set(smallest)
    longest = extent.index(max(extent))
    index_at[longest] = (index_at[longest] + 1) % extent[longest]
    return result.at[tuple(index_at)].set(largest)


def shard_levels(key, dims, split, smallest, top_value):
    loudness, own = 1.0, jax.random.fold_in(key, 6)
    for axis_at, parts in split:
        heights = jnp.exp(jax.random.uniform(jax.random.fold_in(own, axis_at), (parts,), jnp.float32, smallest / len(split), top_value / len(split)))
        loudness = loudness * jnp.repeat(heights, dims[axis_at] // parts).reshape([-1 if axis == axis_at else 1 for axis in range(len(dims))])
    return loudness


def split_up(number_of, total, most, slope):
    portions = [(1 << 20) // math.isqrt(rank ** slope) + 1 for rank in range(2, number_of + 1)]
    spare, counts = total - most - (number_of - 1), [1] * (number_of - 1)
    while spare > 0:
        movable = [i for i in range(number_of - 1) if counts[i] < most]
        whole, remaining = sum([portions[i] for i in movable]), spare
        for i in movable:
            addition = min(most - counts[i], max(1, remaining * portions[i] // whole), spare)
            counts[i] = counts[i] + addition
            spare = spare - addition
    return np.array([most] + counts)


def ragged(key, number_of, total, reach, slope):
    if number_of == 2:
        one = jax.random.randint(key, (), max(1, total - reach), min(reach, total - 1) + 1)
        return jnp.stack([one, total - one])
    tallies = jnp.asarray(split_up(number_of, total, reach, slope), jnp.int32)
    couples = (number_of - 1) // 2
    donor, receiver = tallies[1:1 + 2 * couples:2], tallies[2:2 + 2 * couples:2]
    room = jnp.minimum(donor - 1, reach - receiver)
    passed = jax.random.randint(jax.random.fold_in(key, 1), (couples,), 0, 1 << 20) % (room + 1)
    tallies = tallies.at[1:1 + 2 * couples:2].set(donor - passed).at[2:2 + 2 * couples:2].set(receiver + passed)
    return tallies[jax.random.permutation(jax.random.fold_in(key, 2), number_of)]


def bell_draw(key, shape, width, most, pieces=(), held_as=jnp.bfloat16):
    factor_of = shard_levels(key, shape, pieces, -0.22, 0.18) if pieces else 1.0
    entries = jax.random.normal(key, shape, jnp.float32) * width * factor_of
    return jnp.minimum(jnp.maximum(entries, -most), most).astype(held_as)


def setup_inputs(seed: int = 0) -> dict:
    keys = jax.random.split(jax.random.key(seed), 10)
    return {
        "hidden_acts": bell_draw(keys[0], (TOKENS, FF), 1.0, 6.0, ((0, 8), (1, 16))),
        "out_grads": bell_draw(keys[1], (TOKENS, D), 1.0, 6.0, ((0, 8), (1, 16))),
        "proj_in": bell_draw(keys[2], (FF, SK), FF ** -0.5, 0.03125, ((0, 16),)),
        "proj_out": bell_draw(keys[3], (D, SK), D ** -0.5, 0.0625, ((0, 16),)),
        "white_in": bell_draw(keys[4], (SK, SK), SK ** -0.5, 0.75, (), jnp.float32),
        "white_out": bell_draw(keys[5], (SK, SK), SK ** -0.5, 0.75, (), jnp.float32),
        "ep_lengths": jax.vmap(lambda own: ragged(own, EP_DEV, TOK_DEV, MOST, 1))(jax.random.split(keys[6], N_COL)).reshape((N_COL, EP_DEV)).astype(jnp.int32),
        "flag_ids": place_ends(jax.random.randint(keys[7], (FLAGGED,), 0, EPISODES), jax.random.fold_in(keys[7], 1), 0, EPISODES - 1).astype(jnp.int32),
        "train_sketch": bell_draw(keys[8], (TRAIN, SK * SK), 0.002, 0.01171875, ((0, 16), (1, 8))),
    }


def block_sketch(args):
    out_proj, in_proj, lengths_row = args
    stops_at = jnp.cumsum(lengths_row)
    starts = stops_at - lengths_row
    positions = jnp.arange(TOK_DEV, dtype=jnp.int32)
    member = ((positions[None, :] >= starts[:, None]) & (positions[None, :] < stops_at[:, None])).astype(jnp.float32)
    masked = member[:, :, None] * out_proj[None, :, :]
    sketch = jnp.einsum("eto,ti->eoi", masked, in_proj, precision=lax.Precision.HIGHEST)
    return sketch.reshape(lengths_row.shape[0], SK * SK)


def reference(hidden_acts, out_grads, proj_in, proj_out, white_in, white_out, ep_lengths, flag_ids, train_sketch):
    gproj = jnp.dot(out_grads, proj_out, preferred_element_type=jnp.float32)
    hproj = jnp.dot(hidden_acts, proj_in, preferred_element_type=jnp.float32)
    sketch = lax.map(block_sketch, (gproj.reshape(N_COL, TOK_DEV, SK), hproj.reshape(N_COL, TOK_DEV, SK), ep_lengths))
    sketch = sketch.reshape(EPISODES, SK, SK)
    left_side = jnp.einsum("ab,ebc->eac", white_out, sketch, precision=lax.Precision.HIGHEST)
    whitened = jnp.einsum("eac,dc->ead", left_side, white_in, precision=lax.Precision.HIGHEST)
    whitened = whitened.reshape(EPISODES, SK * SK).astype(jnp.bfloat16)
    queries = jnp.take(whitened, flag_ids, axis=0)
    return jnp.einsum("fk,tk->ft", queries, train_sketch, preferred_element_type=jnp.float32)
```

```python
import jax
import jax.numpy as jnp
from jax import lax
from jax.experimental import pallas as pl
from jax.experimental.pallas import tpu as pltpu
from jax.sharding import PartitionSpec as P

MESH = pl.DeviceIdType.MESH
F32 = jnp.float32
BF16 = jnp.bfloat16
NT = (((1,), (1,)), ((), ()))
NN = (((1,), (0,)), ((), ()))
CHUNKS = 8


def hdot(a, b, dims):
    return lax.dot_general(a, b, dims, precision=lax.Precision.HIGHEST, preferred_element_type=F32)


def windows(lens, flags, g_ref, h_ref, out_ref, starts):
    col = lax.axis_index("col")

    def count(k, total):
        starts[k] = total
        return total + lens[0, k]

    lax.fori_loop(0, 64, count, jnp.int32(0))
    lane = lax.broadcasted_iota(jnp.int32, (64, 128), 1)

    def place(f):
        k = flags[f] - 64 * col
        inside = (k >= 0) & (k < 64)
        k = jnp.where(inside, k, 0)
        return starts[k], jnp.where(inside, lens[0, k], 0)

    def window(ref, start, at):
        first = start // 128
        off = start - first * 128
        a = ref[:, pl.ds(pl.multiple_of(first * 128, 128), 128)]
        second = jnp.minimum(first + 1, 15)
        b = ref[:, pl.ds(pl.multiple_of(second * 128, 128), 128)]
        shift = (at + 128 - off) % 128
        a = pltpu.roll(a, shift, 1)
        b = pltpu.roll(b, shift, 1)
        return jnp.where(lane - at + off < 128, a, b)

    def pair(j, _):
        sa, la = place(2 * j)
        sb, lb = place(2 * j + 1)
        keep = lane < jnp.where(lane < 64, la, lb + 64)
        for at, ref in ((0, g_ref), (64, h_ref)):
            both = jnp.where(lane < 64, window(ref, sa, 0), window(ref, sb, 64))
            out_ref[j, pl.ds(at, 64), :] = jnp.where(keep, both, 0.0)
        return 0

    lax.fori_loop(0, 32, pair, 0)


def kernel(
    w_ref, wi_ref, wo_ref, train_hbm, out_ref,
    train, acc, got, peers, rows, mix, tiles_out, tiles_in, mine, every, query,
    part, send, recv,
    t_sem, w_sem, s0, r0, s1, r1, s2, r2, s3, r3, s4, r4,
):
    row = lax.axis_index("row")
    col = lax.axis_index("col")
    chip = row // 2
    core = row % 2
    n_train = train.shape[0]
    half = n_train // 2
    width = half // CHUNKS
    block = n_train // CHUNKS

    def fetch(k):
        at = pl.ds(k * block, block)
        return pltpu.make_async_copy(train_hbm.at[at, :], train.at[at, :], t_sem.at[k])

    def keep(q):
        return pltpu.make_async_copy(w_ref.at[pl.ds(4 * q + 2 * core, 2)], acc.at[q], w_sem.at[q])

    barrier = pltpu.get_barrier_semaphore()
    for d in range(1, 16):
        pl.semaphore_signal(barrier, inc=1, device_id={"row": (row + d) % 16}, device_id_type=MESH)
    for d in range(1, 8):
        pl.semaphore_signal(barrier, inc=1, device_id={"col": (col + d) % 8}, device_id_type=MESH)

    def copy0(q):
        return pltpu.make_async_remote_copy(
            src_ref=w_ref.at[pl.ds(4 * q + 2 * (1 - core), 2)], dst_ref=got.at[q], send_sem=s0.at[q], recv_sem=r0.at[q],
            device_id={"row": row + 1 - 2 * core}, device_id_type=MESH)

    def copy1(d):
        q = (chip + d) % 8
        return pltpu.make_async_remote_copy(
            src_ref=acc.at[q], dst_ref=peers.at[d - 1], send_sem=s1.at[d - 1], recv_sem=r1.at[d - 1],
            device_id={"row": 2 * q + core}, device_id_type=MESH)

    def copy2(d):
        c = (col + d) % 8
        return pltpu.make_async_remote_copy(
            src_ref=tiles_out.at[c], dst_ref=tiles_in.at[d - 1], send_sem=s2.at[d - 1], recv_sem=r2.at[d - 1],
            device_id={"col": c}, device_id_type=MESH)

    def copy3(d):
        return pltpu.make_async_remote_copy(
            src_ref=mine, dst_ref=every.at[row], send_sem=s3.at[d - 1], recv_sem=r3.at[d - 1],
            device_id={"row": (row + d) % 16}, device_id_type=MESH)

    def copy4(d, j):
        c = (col + d) % 8
        at = pl.ds(pl.multiple_of(j * width, width), width)
        return pltpu.make_async_remote_copy(
            src_ref=send.at[c, :, at], dst_ref=recv.at[d - 1, :, at],
            send_sem=s4.at[d - 1, j], recv_sem=r4.at[d - 1, j],
            device_id={"col": c}, device_id_type=MESH)

    pl.semaphore_wait(barrier, 22)

    for d in (4, 3, 5, 2, 6, 1, 7, 0):
        copy0((chip + d) % 8).start()
    for q in range(8):
        keep(q).start()
    for k in range(CHUNKS):
        fetch(k).start()
    for q in range(8):
        keep(q).wait()
    for d in (4, 3, 5, 2, 6, 1, 7, 0):
        q = (chip + d) % 8
        copy0(q).wait_recv()
        acc[q] = acc[q] + got[q]
        if d:
            copy1(d).start()
    for d in (1, 7, 2, 6, 3, 5, 4):
        copy1(d).wait_recv()

    for p in range(2):
        total = acc[chip, p]
        for d in range(7):
            total = total + peers[d, p]
        mix[...] = hdot(wo_ref[...], total[:64], NN)
        hw = hdot(wi_ref[...], total[64:], NN)
        hw = jnp.concatenate([hw, hw], axis=0)
        even = mix[pl.ds(0, 32, 2), :]
        odd = mix[pl.ds(1, 32, 2), :]
        low = lax.broadcasted_iota(jnp.int32, (32, 128), 1) < 64
        for u in range(2):
            if u == 0:
                ev, od = jnp.where(low, even, 0.0), jnp.where(low, odd, 0.0)
            else:
                ev, od = jnp.where(low, 0.0, even), jnp.where(low, 0.0, odd)
            qe = hdot(ev, hw, NT)
            qo = hdot(od, hw, NT)
            rows[pl.ds(2 * p + u, 32, 4), :] = jnp.where(low, qe, qo)
    tiles_out[...] = rows[...].astype(BF16).reshape(8, 16, 128)
    for d in range(1, 8):
        copy2(d).start()
    tile = tiles_out[col].astype(F32)
    for d in range(1, 8):
        copy2(d).wait_recv()
        tile = tile + tiles_in[d - 1].astype(F32)
    tile = tile.astype(BF16)
    mine[...] = tile
    for d in range(1, 16):
        copy3(d).start()
    every[row] = tile
    for d in range(1, 16):
        copy3(d).wait_recv()

    flat = every[...].reshape(256, 128)
    to = lax.broadcasted_iota(jnp.int32, (64, 256), 0)
    frm = lax.broadcasted_iota(jnp.int32, (64, 256), 1)
    for a in range(4):
        perm = jnp.where(frm == (to // 4) * 16 + 4 * a + to % 4, 1.0, 0.0).astype(BF16)
        query[:, 128 * a:128 * (a + 1)] = lax.dot_general(perm, flat, NN, preferred_element_type=F32).astype(BF16)

    for k in range(CHUNKS):
        fetch(k).wait()

    def score(j, _):
        lo = pl.multiple_of(j * width, width)
        hi = pl.multiple_of(half + j * width, width)
        own = pl.ds(pl.multiple_of(col * 8, 8), 8)
        a = lax.dot_general(query[...], train[pl.ds(lo, width), :], NT, preferred_element_type=F32)
        b = lax.dot_general(query[...], train[pl.ds(hi, width), :], NT, preferred_element_type=F32)
        for c in range(8):
            both = jnp.concatenate([a[8 * c:8 * c + 8], b[8 * c:8 * c + 8]], axis=0)
            send[c, :, pl.ds(lo, width)] = both.astype(BF16)
        for d in (4, 3, 5, 2, 6, 1, 7):
            copy4(d, j).start()
        part[...] = a
        out_ref[:, pl.ds(lo, width)] = part[own, :]
        part[...] = b
        out_ref[:, pl.ds(hi, width)] = part[own, :]
        return 0

    lax.fori_loop(0, CHUNKS, score, 0)

    def collect(j, _):
        lo = pl.ds(pl.multiple_of(j * width, width), width)
        hi = pl.ds(pl.multiple_of(half + j * width, width), width)
        both = jnp.concatenate([out_ref[:, lo], out_ref[:, hi]], axis=0)
        for d in range(1, 8):
            copy4(d, j).wait_recv()
            both = both + recv[d - 1, :, lo].astype(F32)
        out_ref[:, lo] = both[:8]
        out_ref[:, hi] = both[8:]
        return 0

    lax.fori_loop(0, CHUNKS, collect, 0)

    def sent0(q, _):
        copy0(q).wait_send()
        return 0

    lax.fori_loop(0, 8, sent0, 0)
    for d in range(1, 8):
        copy1(d).wait_send()
        copy2(d).wait_send()
    for d in range(1, 16):
        copy3(d).wait_send()

    def sent4(j, _):
        for d in range(1, 8):
            copy4(d, j).wait_send()
        return 0

    lax.fori_loop(0, CHUNKS, sent4, 0)


def on_device(hidden_acts, out_grads, proj_in, proj_out, white_in, white_out, ep_lengths, flag_ids, train_sketch):
    across = (((0,), (1,)), ((), ()))
    g_t = lax.dot_general(proj_out, out_grads, across, preferred_element_type=F32)
    h_t = lax.dot_general(proj_in, hidden_acts, across, preferred_element_type=F32)
    n_train, depth = train_sketch.shape
    vmem = pl.BlockSpec(memory_space=pltpu.VMEM)
    smem = pl.BlockSpec(memory_space=pltpu.SMEM)
    dma = pltpu.SemaphoreType.DMA
    w = pl.pallas_call(
        windows,
        out_shape=jax.ShapeDtypeStruct((32, 128, 128), F32),
        in_specs=[smem, smem, vmem, vmem],
        out_specs=vmem,
        scratch_shapes=[pltpu.SMEM((64,), jnp.int32)],
        name="windows",
    )(ep_lengths, flag_ids, g_t, h_t)
    hbm = pl.BlockSpec(memory_space=pl.ANY)
    return pl.pallas_call(
        kernel,
        out_shape=jax.ShapeDtypeStruct((8, n_train), F32),
        in_specs=[hbm, vmem, vmem, hbm],
        out_specs=vmem,
        scratch_shapes=[
            pltpu.VMEM((n_train, depth), BF16),
            pltpu.VMEM((8, 2, 128, 128), F32),
            pltpu.VMEM((8, 2, 128, 128), F32),
            pltpu.VMEM((7, 2, 128, 128), F32),
            pltpu.VMEM((128, 128), F32),
            pltpu.VMEM((64, 128), F32),
            pltpu.VMEM((8, 16, 128), BF16),
            pltpu.VMEM((7, 16, 128), BF16),
            pltpu.VMEM((16, 128), BF16),
            pltpu.VMEM((16, 16, 128), BF16),
            pltpu.VMEM((64, depth), BF16),
            pltpu.VMEM((64, n_train // 2 // CHUNKS), F32),
            pltpu.VMEM((8, 16, n_train // 2), BF16),
            pltpu.VMEM((7, 16, n_train // 2), BF16),
            dma((CHUNKS,)), dma((8,)),
            dma((8,)), dma((8,)),
            dma((7,)), dma((7,)),
            dma((7,)), dma((7,)),
            dma((15,)), dma((15,)),
            dma((7, CHUNKS)), dma((7, CHUNKS)),
        ],
        compiler_params=pltpu.CompilerParams(collective_id=0, has_side_effects=True),
        name="attribute",
    )(w, white_in, white_out, train_sketch)


def solution(mesh):
    in_specs = (
        P("col", "row"), P("col", "row"), P("row", None), P("row", None), P(), P(),
        P("col", None), P(), P("row", "col"),
    )
    return jax.shard_map(on_device, mesh=mesh, in_specs=in_specs, out_specs=P("col", "row"), check_vma=False)
```

```python
import jax
import jax.numpy as jnp
from jax import lax
from jax.experimental import pallas as pl
from jax.experimental.pallas import tpu as pltpu
from jax.sharding import PartitionSpec as P

MESH = pl.DeviceIdType.MESH
F32 = jnp.float32
BF16 = jnp.bfloat16
NT = (((1,), (1,)), ((), ()))
NN = (((1,), (0,)), ((), ()))
CHUNKS = 8


def hdot(a, b, dims):
    return lax.dot_general(a, b, dims, precision=lax.Precision.HIGHEST, preferred_element_type=F32)


def windows(lens, flags, pin_ref, pout_ref, acts_hbm, grads_hbm, out_ref, starts, acts, grads, gh, a_sem, g_sem):
    col = lax.axis_index("col")
    few = acts.shape[2]
    tokens = CHUNKS * few

    def bring(k):
        at = pl.ds(k * few, few)
        return (pltpu.make_async_copy(acts_hbm.at[:, at], acts.at[k], a_sem.at[k]),
                pltpu.make_async_copy(grads_hbm.at[at, :], grads.at[at, :], g_sem.at[k]))

    for k in range(CHUNKS):
        for copy in bring(k):
            copy.start()

    def count(k, total):
        starts[k] = total
        return total + lens[0, k]

    lax.fori_loop(0, 64, count, jnp.int32(0))
    gh[pl.ds(tokens, 64), :] = jnp.zeros((64, 128), F32)

    for k in range(CHUNKS):
        for copy in bring(k):
            copy.wait()
        at = pl.ds(k * few, few)
        g = lax.dot_general(pout_ref[...], grads[at, :], NT, preferred_element_type=F32)
        h = lax.dot_general(pin_ref[...], acts[k], NN, preferred_element_type=F32)
        gh[at, :] = jnp.concatenate([g, h], axis=0).T

    token = lax.broadcasted_iota(jnp.int32, (64, 128), 0)

    def window(f):
        k = flags[f] - 64 * col
        inside = (k >= 0) & (k < 64)
        k = jnp.where(inside, k, 0)
        n = jnp.where(inside, lens[0, k], 0)
        return jnp.where(token < n, gh[pl.ds(starts[k], 64), :], 0.0)

    def pair(j, _):
        for u in range(2):
            out_ref[j, pl.ds(64 * u, 64), :] = window(2 * j + u)
        return 0

    lax.fori_loop(0, 32, pair, 0, unroll=4)


def kernel(
    w_ref, wi_ref, wo_ref, train_hbm, out_ref,
    train, acc, got, peers, rows, tiles_out, tiles_in, mine, every, query,
    part, send, recv,
    t_sem, w_sem, s0, r0, s1, r1, s2, r2, s3, r3, s4, r4,
):
    row = lax.axis_index("row")
    col = lax.axis_index("col")
    chip = row // 2
    core = row % 2
    n_train = train.shape[0]
    half = n_train // 2
    width = half // CHUNKS
    block = n_train // CHUNKS

    def fetch(k):
        at = pl.ds(k * block, block)
        return pltpu.make_async_copy(train_hbm.at[at, :], train.at[at, :], t_sem.at[k])

    def keep(q):
        return pltpu.make_async_copy(w_ref.at[pl.ds(4 * q + 2 * core, 2)], acc.at[q], w_sem.at[q])

    barrier = pltpu.get_barrier_semaphore()
    for d in range(1, 16):
        pl.semaphore_signal(barrier, inc=1, device_id={"row": (row + d) % 16}, device_id_type=MESH)
    for d in range(1, 8):
        pl.semaphore_signal(barrier, inc=1, device_id={"col": (col + d) % 8}, device_id_type=MESH)

    def copy0(q):
        return pltpu.make_async_remote_copy(
            src_ref=w_ref.at[pl.ds(4 * q + 2 * (1 - core), 2)], dst_ref=got.at[q], send_sem=s0.at[q], recv_sem=r0.at[q],
            device_id={"row": row + 1 - 2 * core}, device_id_type=MESH)

    def copy1(d):
        q = (chip + d) % 8
        return pltpu.make_async_remote_copy(
            src_ref=acc.at[q], dst_ref=peers.at[d - 1], send_sem=s1.at[d - 1], recv_sem=r1.at[d - 1],
            device_id={"row": 2 * q + core}, device_id_type=MESH)

    def copy2(d):
        c = (col + d) % 8
        return pltpu.make_async_remote_copy(
            src_ref=tiles_out.at[c], dst_ref=tiles_in.at[d - 1], send_sem=s2.at[d - 1], recv_sem=r2.at[d - 1],
            device_id={"col": c}, device_id_type=MESH)

    def copy3(d):
        return pltpu.make_async_remote_copy(
            src_ref=mine, dst_ref=every.at[row], send_sem=s3.at[d - 1], recv_sem=r3.at[d - 1],
            device_id={"row": (row + d) % 16}, device_id_type=MESH)

    def copy4(d, j):
        c = (col + d) % 8
        at = pl.ds(pl.multiple_of(j * width, width), width)
        return pltpu.make_async_remote_copy(
            src_ref=send.at[c, :, at], dst_ref=recv.at[d - 1, :, at],
            send_sem=s4.at[d - 1, j], recv_sem=r4.at[d - 1, j],
            device_id={"col": c}, device_id_type=MESH)

    pl.semaphore_wait(barrier, 22)

    for d in (4, 3, 5, 2, 6, 1, 7, 0):
        copy0((chip + d) % 8).start()
    for q in range(8):
        keep(q).start()
    for k in range(CHUNKS):
        fetch(k).start()
    for q in range(8):
        keep(q).wait()
    for d in (4, 3, 5, 2, 6, 1, 7, 0):
        q = (chip + d) % 8
        copy0(q).wait_recv()
        acc[q] = acc[q] + got[q]
        if d:
            copy1(d).start()
    for d in (1, 7, 2, 6, 3, 5, 4):
        copy1(d).wait_recv()

    none = jnp.zeros((64, 64), F32)
    wi = jnp.concatenate([none, wi_ref[...]], axis=1)
    wi = jnp.concatenate([wi, wi], axis=0)
    wo = jnp.concatenate([wo_ref[pl.ds(0, 32, 2), :], wo_ref[pl.ds(1, 32, 2), :]], axis=0)
    wo = jnp.concatenate([wo, none], axis=1)
    low = lax.broadcasted_iota(jnp.int32, (64, 128), 1) < 64
    for p in range(2):
        total = acc[chip, p]
        for d in range(7):
            total = total + peers[d, p]
        gw = hdot(wo, total, NT)
        hw = hdot(total, wi, NT)
        for u in range(2):
            both = hdot(jnp.where(low if u == 0 else ~low, gw, 0.0), hw, NN)
            rows[pl.ds(2 * p + u, 32, 4), :] = jnp.where(low[:32], both[:32], both[32:])
    tiles_out[...] = rows[...].astype(BF16).reshape(8, 16, 128)
    for d in range(1, 8):
        copy2(d).start()
    tile = tiles_out[col].astype(F32)
    for d in range(1, 8):
        copy2(d).wait_recv()
        tile = tile + tiles_in[d - 1].astype(F32)
    tile = tile.astype(BF16)
    mine[...] = tile
    for d in range(1, 16):
        copy3(d).start()
    every[row] = tile
    for d in range(1, 16):
        copy3(d).wait_recv()

    flat = every[...].reshape(256, 128)
    to = lax.broadcasted_iota(jnp.int32, (64, 256), 0)
    frm = lax.broadcasted_iota(jnp.int32, (64, 256), 1)
    for a in range(4):
        perm = jnp.where(frm == (to // 4) * 16 + 4 * a + to % 4, 1.0, 0.0).astype(BF16)
        query[:, 128 * a:128 * (a + 1)] = lax.dot_general(perm, flat, NN, preferred_element_type=F32).astype(BF16)

    for k in range(CHUNKS):
        fetch(k).wait()

    def score(j, _):
        lo = pl.multiple_of(j * width, width)
        hi = pl.multiple_of(half + j * width, width)
        own = pl.ds(pl.multiple_of(col * 8, 8), 8)
        a = lax.dot_general(query[...], train[pl.ds(lo, width), :], NT, preferred_element_type=F32)
        b = lax.dot_general(query[...], train[pl.ds(hi, width), :], NT, preferred_element_type=F32)
        for c in range(8):
            both = jnp.concatenate([a[8 * c:8 * c + 8], b[8 * c:8 * c + 8]], axis=0)
            send[c, :, pl.ds(lo, width)] = both.astype(BF16)
        for d in (4, 3, 5, 2, 6, 1, 7):
            copy4(d, j).start()
        part[...] = a
        out_ref[:, pl.ds(lo, width)] = part[own, :]
        part[...] = b
        out_ref[:, pl.ds(hi, width)] = part[own, :]
        return 0

    lax.fori_loop(0, CHUNKS, score, 0)

    def collect(j, _):
        lo = pl.ds(pl.multiple_of(j * width, width), width)
        hi = pl.ds(pl.multiple_of(half + j * width, width), width)
        both = jnp.concatenate([out_ref[:, lo], out_ref[:, hi]], axis=0)
        for d in range(1, 8):
            copy4(d, j).wait_recv()
            both = both + recv[d - 1, :, lo].astype(F32)
        out_ref[:, lo] = both[:8]
        out_ref[:, hi] = both[8:]
        return 0

    lax.fori_loop(0, CHUNKS, collect, 0)

    def sent0(q, _):
        copy0(q).wait_send()
        return 0

    lax.fori_loop(0, 8, sent0, 0)
    for d in range(1, 8):
        copy1(d).wait_send()
        copy2(d).wait_send()
    for d in range(1, 16):
        copy3(d).wait_send()

    def sent4(j, _):
        for d in range(1, 8):
            copy4(d, j).wait_send()
        return 0

    lax.fori_loop(0, CHUNKS, sent4, 0)


def on_device(hidden_acts, out_grads, proj_in, proj_out, white_in, white_out, ep_lengths, flag_ids, train_sketch):
    tokens, width = hidden_acts.shape
    model = out_grads.shape[1]
    n_train, depth = train_sketch.shape
    vmem = pl.BlockSpec(memory_space=pltpu.VMEM)
    smem = pl.BlockSpec(memory_space=pltpu.SMEM)
    dma = pltpu.SemaphoreType.DMA
    hbm = pl.BlockSpec(memory_space=pl.ANY)
    w = pl.pallas_call(
        windows,
        out_shape=jax.ShapeDtypeStruct((32, 128, 128), F32),
        in_specs=[smem, smem, vmem, vmem, hbm, hbm],
        out_specs=vmem,
        scratch_shapes=[
            pltpu.SMEM((64,), jnp.int32),
            pltpu.VMEM((CHUNKS, width, tokens // CHUNKS), BF16),
            pltpu.VMEM((tokens, model), BF16),
            pltpu.VMEM((tokens + 64, 128), F32),
            dma((CHUNKS,)), dma((CHUNKS,)),
        ],
        name="windows",
    )(ep_lengths, flag_ids, proj_in.T, proj_out.T, hidden_acts.T, out_grads)
    return pl.pallas_call(
        kernel,
        out_shape=jax.ShapeDtypeStruct((8, n_train), F32),
        in_specs=[hbm, vmem, vmem, hbm],
        out_specs=vmem,
        scratch_shapes=[
            pltpu.VMEM((n_train, depth), BF16),
            pltpu.VMEM((8, 2, 128, 128), F32),
            pltpu.VMEM((8, 2, 128, 128), F32),
            pltpu.VMEM((7, 2, 128, 128), F32),
            pltpu.VMEM((128, 128), F32),
            pltpu.VMEM((8, 16, 128), BF16),
            pltpu.VMEM((7, 16, 128), BF16),
            pltpu.VMEM((16, 128), BF16),
            pltpu.VMEM((16, 16, 128), BF16),
            pltpu.VMEM((64, depth), BF16),
            pltpu.VMEM((64, n_train // 2 // CHUNKS), F32),
            pltpu.VMEM((8, 16, n_train // 2), BF16),
            pltpu.VMEM((7, 16, n_train // 2), BF16),
            dma((CHUNKS,)), dma((8,)),
            dma((8,)), dma((8,)),
            dma((7,)), dma((7,)),
            dma((7,)), dma((7,)),
            dma((15,)), dma((15,)),
            dma((7, CHUNKS)), dma((7, CHUNKS)),
        ],
        compiler_params=pltpu.CompilerParams(collective_id=0, has_side_effects=True),
        name="attribute",
    )(w, white_in, white_out, train_sketch)


def solution(mesh):
    in_specs = (
        P("col", "row"), P("col", "row"), P("row", None), P("row", None), P(), P(),
        P("col", None), P(), P("row", "col"),
    )
    return jax.shard_map(on_device, mesh=mesh, in_specs=in_specs, out_specs=P("col", "row"), check_vma=False)
```

```python
import jax
import jax.numpy as jnp
from jax import lax
from jax.experimental import pallas as pl
from jax.experimental.pallas import tpu as pltpu
from jax.sharding import PartitionSpec as P

MESH = pl.DeviceIdType.MESH
F32 = jnp.float32
BF16 = jnp.bfloat16
NT = (((1,), (1,)), ((), ()))
NN = (((1,), (0,)), ((), ()))
CHUNKS = 8


def hdot(a, b, dims):
    return lax.dot_general(a, b, dims, precision=lax.Precision.HIGHEST, preferred_element_type=F32)


def windows(lens, flags, pin_ref, pout_ref, acts_hbm, grads_hbm, out_ref, starts, acts, grads, gh, a_sem, g_sem):
    col = lax.axis_index("col")
    few = acts.shape[2]
    tokens = CHUNKS * few

    def bring(k):
        at = pl.ds(k * few, few)
        return (pltpu.make_async_copy(acts_hbm.at[:, at], acts.at[k], a_sem.at[k]),
                pltpu.make_async_copy(grads_hbm.at[at, :], grads.at[at, :], g_sem.at[k]))

    for k in range(CHUNKS):
        for copy in bring(k):
            copy.start()

    def count(k, total):
        starts[k] = total
        return total + lens[0, k]

    lax.fori_loop(0, 64, count, jnp.int32(0))
    gh[pl.ds(tokens, 64), :] = jnp.zeros((64, 128), F32)

    for k in range(CHUNKS):
        for copy in bring(k):
            copy.wait()
        at = pl.ds(k * few, few)
        g = lax.dot_general(pout_ref[...], grads[at, :], NT, preferred_element_type=F32)
        h = lax.dot_general(pin_ref[...], acts[k], NN, preferred_element_type=F32)
        gh[at, :] = jnp.concatenate([g, h], axis=0).T

    token = lax.broadcasted_iota(jnp.int32, (64, 128), 0)

    def window(f):
        k = flags[f] - 64 * col
        inside = (k >= 0) & (k < 64)
        k = jnp.where(inside, k, 0)
        n = jnp.where(inside, lens[0, k], 0)
        return jnp.where(token < n, gh[pl.ds(starts[k], 64), :], 0.0)

    def pair(j, _):
        for u in range(2):
            out_ref[j, pl.ds(64 * u, 64), :] = window(2 * j + u)
        return 0

    lax.fori_loop(0, 32, pair, 0, unroll=4)


def kernel(
    w_ref, wi_ref, wo_ref, train_hbm, out_ref,
    train, acc, got, coded, unit, codes, units, rows, tiles_out, tiles_in, mine, every, query,
    part, send, recv,
    t_sem, w_sem, s0, r0, s1, r1, s5, r5, s2, r2, s3, r3, s4, r4,
):
    row = lax.axis_index("row")
    col = lax.axis_index("col")
    chip = row // 2
    core = row % 2
    n_train = train.shape[0]
    half = n_train // 2
    width = half // CHUNKS
    block = n_train // CHUNKS

    def fetch(k):
        at = pl.ds(k * block, block)
        return pltpu.make_async_copy(train_hbm.at[at, :], train.at[at, :], t_sem.at[k])

    def keep(q):
        return pltpu.make_async_copy(w_ref.at[pl.ds(4 * q + 2 * core, 2)], acc.at[q], w_sem.at[q])

    barrier = pltpu.get_barrier_semaphore()
    for d in range(1, 16):
        pl.semaphore_signal(barrier, inc=1, device_id={"row": (row + d) % 16}, device_id_type=MESH)
    for d in range(1, 8):
        pl.semaphore_signal(barrier, inc=1, device_id={"col": (col + d) % 8}, device_id_type=MESH)

    def copy0(q):
        return pltpu.make_async_remote_copy(
            src_ref=w_ref.at[pl.ds(4 * q + 2 * (1 - core), 2)], dst_ref=got.at[q], send_sem=s0.at[q], recv_sem=r0.at[q],
            device_id={"row": row + 1 - 2 * core}, device_id_type=MESH)

    def copy1(d):
        q = (chip + d) % 8
        return pltpu.make_async_remote_copy(
            src_ref=coded.at[q], dst_ref=codes.at[d - 1], send_sem=s1.at[d - 1], recv_sem=r1.at[d - 1],
            device_id={"row": 2 * q + core}, device_id_type=MESH)

    def copy5(d):
        q = (chip + d) % 8
        return pltpu.make_async_remote_copy(
            src_ref=unit.at[q], dst_ref=units.at[d - 1], send_sem=s5.at[d - 1], recv_sem=r5.at[d - 1],
            device_id={"row": 2 * q + core}, device_id_type=MESH)

    def copy2(d):
        c = (col + d) % 8
        return pltpu.make_async_remote_copy(
            src_ref=tiles_out.at[c], dst_ref=tiles_in.at[d - 1], send_sem=s2.at[d - 1], recv_sem=r2.at[d - 1],
            device_id={"col": c}, device_id_type=MESH)

    def copy3(d):
        return pltpu.make_async_remote_copy(
            src_ref=mine, dst_ref=every.at[row], send_sem=s3.at[d - 1], recv_sem=r3.at[d - 1],
            device_id={"row": (row + d) % 16}, device_id_type=MESH)

    def copy4(d, j):
        c = (col + d) % 8
        at = pl.ds(pl.multiple_of(j * width, width), width)
        return pltpu.make_async_remote_copy(
            src_ref=send.at[c, :, at], dst_ref=recv.at[d - 1, :, at],
            send_sem=s4.at[d - 1, j], recv_sem=r4.at[d - 1, j],
            device_id={"col": c}, device_id_type=MESH)

    pl.semaphore_wait(barrier, 22)

    for d in (4, 3, 5, 2, 6, 1, 7, 0):
        copy0((chip + d) % 8).start()
    for q in range(8):
        keep(q).start()
    for k in range(CHUNKS):
        fetch(k).start()
    for q in range(8):
        keep(q).wait()
    for d in (4, 3, 5, 2, 6, 1, 7, 0):
        q = (chip + d) % 8
        copy0(q).wait_recv()
        if d == 0:
            acc[q] = acc[q] + got[q]
            continue
        for p in range(2):
            for u in range(2):
                at = pl.ds(64 * u, 64)
                both = acc[q, p, at, :] + got[q, p, at, :]
                top = jnp.maximum(jnp.max(jnp.abs(both), axis=0, keepdims=True), 1e-30)
                coded[q, p, at, :] = jnp.round(both * (32767.0 / top)).astype(jnp.int32).astype(jnp.int16)
                unit[q, pl.ds(2 * p + u, 1), :] = top * (1.0 / 32767.0)
        copy1(d).start()
        copy5(d).start()
    for d in (1, 7, 2, 6, 3, 5, 4):
        copy1(d).wait_recv()
        copy5(d).wait_recv()

    none = jnp.zeros((64, 64), F32)
    wi = jnp.concatenate([none, wi_ref[...]], axis=1)
    wi = jnp.concatenate([wi, wi], axis=0)
    wo = jnp.concatenate([wo_ref[pl.ds(0, 32, 2), :], wo_ref[pl.ds(1, 32, 2), :]], axis=0)
    wo = jnp.concatenate([wo, none], axis=1)
    low = lax.broadcasted_iota(jnp.int32, (64, 128), 1) < 64
    for p in range(2):
        total = acc[chip, p]
        for d in range(7):
            part_of = codes[d, p].astype(jnp.int32).astype(F32)
            total = total + jnp.concatenate([
                part_of[:64] * units[d, pl.ds(2 * p, 1), :], part_of[64:] * units[d, pl.ds(2 * p + 1, 1), :]], axis=0)
        gw = hdot(wo, total, NT)
        hw = hdot(total, wi, NT)
        for u in range(2):
            both = hdot(jnp.where(low if u == 0 else ~low, gw, 0.0), hw, NN)
            rows[pl.ds(2 * p + u, 32, 4), :] = jnp.where(low[:32], both[:32], both[32:])
    tiles_out[...] = rows[...].astype(BF16).reshape(8, 16, 128)
    for d in range(1, 8):
        copy2(d).start()
    tile = tiles_out[col].astype(F32)
    for d in range(1, 8):
        copy2(d).wait_recv()
        tile = tile + tiles_in[d - 1].astype(F32)
    tile = tile.astype(BF16)
    mine[...] = tile
    for d in range(1, 16):
        copy3(d).start()
    every[row] = tile
    for d in range(1, 16):
        copy3(d).wait_recv()

    flat = every[...].reshape(256, 128)
    to = lax.broadcasted_iota(jnp.int32, (64, 256), 0)
    frm = lax.broadcasted_iota(jnp.int32, (64, 256), 1)
    for a in range(4):
        perm = jnp.where(frm == (to // 4) * 16 + 4 * a + to % 4, 1.0, 0.0).astype(BF16)
        query[:, 128 * a:128 * (a + 1)] = lax.dot_general(perm, flat, NN, preferred_element_type=F32).astype(BF16)

    for k in range(CHUNKS):
        fetch(k).wait()

    def score(j, _):
        lo = pl.multiple_of(j * width, width)
        hi = pl.multiple_of(half + j * width, width)
        own = pl.ds(pl.multiple_of(col * 8, 8), 8)
        a = lax.dot_general(query[...], train[pl.ds(lo, width), :], NT, preferred_element_type=F32)
        b = lax.dot_general(query[...], train[pl.ds(hi, width), :], NT, preferred_element_type=F32)
        for c in range(8):
            both = jnp.concatenate([a[8 * c:8 * c + 8], b[8 * c:8 * c + 8]], axis=0)
            send[c, :, pl.ds(lo, width)] = both.astype(BF16)
        for d in (4, 3, 5, 2, 6, 1, 7):
            copy4(d, j).start()
        part[...] = a
        out_ref[:, pl.ds(lo, width)] = part[own, :]
        part[...] = b
        out_ref[:, pl.ds(hi, width)] = part[own, :]
        return 0

    lax.fori_loop(0, CHUNKS, score, 0)

    def collect(j, _):
        lo = pl.ds(pl.multiple_of(j * width, width), width)
        hi = pl.ds(pl.multiple_of(half + j * width, width), width)
        both = jnp.concatenate([out_ref[:, lo], out_ref[:, hi]], axis=0)
        for d in range(1, 8):
            copy4(d, j).wait_recv()
            both = both + recv[d - 1, :, lo].astype(F32)
        out_ref[:, lo] = both[:8]
        out_ref[:, hi] = both[8:]
        return 0

    lax.fori_loop(0, CHUNKS, collect, 0)

    def sent0(q, _):
        copy0(q).wait_send()
        return 0

    lax.fori_loop(0, 8, sent0, 0)
    for d in range(1, 8):
        copy1(d).wait_send()
        copy5(d).wait_send()
        copy2(d).wait_send()
    for d in range(1, 16):
        copy3(d).wait_send()

    def sent4(j, _):
        for d in range(1, 8):
            copy4(d, j).wait_send()
        return 0

    lax.fori_loop(0, CHUNKS, sent4, 0)


def on_device(hidden_acts, out_grads, proj_in, proj_out, white_in, white_out, ep_lengths, flag_ids, train_sketch):
    tokens, width = hidden_acts.shape
    model = out_grads.shape[1]
    n_train, depth = train_sketch.shape
    vmem = pl.BlockSpec(memory_space=pltpu.VMEM)
    smem = pl.BlockSpec(memory_space=pltpu.SMEM)
    dma = pltpu.SemaphoreType.DMA
    hbm = pl.BlockSpec(memory_space=pl.ANY)
    w = pl.pallas_call(
        windows,
        out_shape=jax.ShapeDtypeStruct((32, 128, 128), F32),
        in_specs=[smem, smem, vmem, vmem, hbm, hbm],
        out_specs=vmem,
        scratch_shapes=[
            pltpu.SMEM((64,), jnp.int32),
            pltpu.VMEM((CHUNKS, width, tokens // CHUNKS), BF16),
            pltpu.VMEM((tokens, model), BF16),
            pltpu.VMEM((tokens + 64, 128), F32),
            dma((CHUNKS,)), dma((CHUNKS,)),
        ],
        name="windows",
    )(ep_lengths, flag_ids, proj_in.T, proj_out.T, hidden_acts.T, out_grads)
    return pl.pallas_call(
        kernel,
        out_shape=jax.ShapeDtypeStruct((8, n_train), F32),
        in_specs=[hbm, vmem, vmem, hbm],
        out_specs=vmem,
        scratch_shapes=[
            pltpu.VMEM((n_train, depth), BF16),
            pltpu.VMEM((8, 2, 128, 128), F32),
            pltpu.VMEM((8, 2, 128, 128), F32),
            pltpu.VMEM((8, 2, 128, 128), jnp.int16),
            pltpu.VMEM((8, 4, 128), F32),
            pltpu.VMEM((7, 2, 128, 128), jnp.int16),
            pltpu.VMEM((7, 4, 128), F32),
            pltpu.VMEM((128, 128), F32),
            pltpu.VMEM((8, 16, 128), BF16),
            pltpu.VMEM((7, 16, 128), BF16),
            pltpu.VMEM((16, 128), BF16),
            pltpu.VMEM((16, 16, 128), BF16),
            pltpu.VMEM((64, depth), BF16),
            pltpu.VMEM((64, n_train // 2 // CHUNKS), F32),
            pltpu.VMEM((8, 16, n_train // 2), BF16),
            pltpu.VMEM((7, 16, n_train // 2), BF16),
            dma((CHUNKS,)), dma((8,)),
            dma((8,)), dma((8,)),
            dma((7,)), dma((7,)),
            dma((7,)), dma((7,)),
            dma((7,)), dma((7,)),
            dma((15,)), dma((15,)),
            dma((7, CHUNKS)), dma((7, CHUNKS)),
        ],
        compiler_params=pltpu.CompilerParams(collective_id=0, has_side_effects=True),
        name="attribute",
    )(w, white_in, white_out, train_sketch)


def solution(mesh):
    in_specs = (
        P("col", "row"), P("col", "row"), P("row", None), P("row", None), P(), P(),
        P("col", None), P(), P("row", "col"),
    )
    return jax.shard_map(on_device, mesh=mesh, in_specs=in_specs, out_specs=P("col", "row"), check_vma=False)
```

```python
import jax
import jax.numpy as jnp
from jax import lax
from jax.experimental import pallas as pl
from jax.experimental.pallas import tpu as pltpu
from jax.sharding import PartitionSpec as P

MESH = pl.DeviceIdType.MESH
F32 = jnp.float32
BF16 = jnp.bfloat16
NT = (((1,), (1,)), ((), ()))
NN = (((1,), (0,)), ((), ()))
CHUNKS = 4


def hdot(a, b, dims):
    return lax.dot_general(a, b, dims, precision=lax.Precision.HIGHEST, preferred_element_type=F32)


def windows(lens, flags, pin_ref, pout_ref, acts_hbm, grads_hbm, out_ref, starts, acts, grads, gh, a_sem, g_sem):
    col = lax.axis_index("col")
    few = acts.shape[2]
    tokens = CHUNKS * few

    def bring(k):
        at = pl.ds(k * few, few)
        return (pltpu.make_async_copy(acts_hbm.at[:, at], acts.at[k], a_sem.at[k]),
                pltpu.make_async_copy(grads_hbm.at[at, :], grads.at[at, :], g_sem.at[k]))

    for k in range(CHUNKS):
        for copy in bring(k):
            copy.start()

    def count(k, total):
        starts[k] = total
        return total + lens[0, k]

    lax.fori_loop(0, 64, count, jnp.int32(0))
    gh[pl.ds(tokens, 64), :] = jnp.zeros((64, 128), F32)

    for k in range(CHUNKS):
        for copy in bring(k):
            copy.wait()
        at = pl.ds(k * few, few)
        g = lax.dot_general(pout_ref[...], grads[at, :], NT, preferred_element_type=F32)
        h = lax.dot_general(pin_ref[...], acts[k], NN, preferred_element_type=F32)
        gh[at, :] = jnp.concatenate([g, h], axis=0).T

    token = lax.broadcasted_iota(jnp.int32, (64, 128), 0)

    def window(f):
        k = flags[f] - 64 * col
        inside = (k >= 0) & (k < 64)
        k = jnp.where(inside, k, 0)
        n = jnp.where(inside, lens[0, k], 0)
        return jnp.where(token < n, gh[pl.ds(starts[k], 64), :], 0.0)

    def pair(j, _):
        for u in range(2):
            out_ref[j, pl.ds(64 * u, 64), :] = window(2 * j + u)
        return 0

    lax.fori_loop(0, 32, pair, 0, unroll=16)


def kernel(
    w_ref, wi_ref, wo_ref, train_hbm, out_ref,
    train, acc, got, coded, unit, codes, units, rows, tiles_out, tiles_in, mine, every, query,
    part, send, recv,
    t_sem, w_sem, s0, r0, s1, r1, s5, r5, s2, r2, s3, r3, s4, r4,
):
    row = lax.axis_index("row")
    col = lax.axis_index("col")
    chip = row // 2
    core = row % 2
    n_train = train.shape[0]
    half = n_train // 2
    width = half // CHUNKS
    block = n_train // CHUNKS

    def fetch(k):
        at = pl.ds(k * block, block)
        return pltpu.make_async_copy(train_hbm.at[at, :], train.at[at, :], t_sem.at[k])

    def keep(q):
        return pltpu.make_async_copy(w_ref.at[pl.ds(4 * q + 2 * core, 2)], acc.at[q], w_sem.at[q])

    barrier = pltpu.get_barrier_semaphore()
    for d in range(1, 16):
        pl.semaphore_signal(barrier, inc=1, device_id={"row": (row + d) % 16}, device_id_type=MESH)
    for d in range(1, 8):
        pl.semaphore_signal(barrier, inc=1, device_id={"col": (col + d) % 8}, device_id_type=MESH)

    def copy0(q):
        return pltpu.make_async_remote_copy(
            src_ref=w_ref.at[pl.ds(4 * q + 2 * (1 - core), 2)], dst_ref=got.at[q], send_sem=s0.at[q], recv_sem=r0.at[q],
            device_id={"row": row + 1 - 2 * core}, device_id_type=MESH)

    def copy1(d):
        q = (chip + d) % 8
        return pltpu.make_async_remote_copy(
            src_ref=coded.at[q], dst_ref=codes.at[d - 1], send_sem=s1.at[d - 1], recv_sem=r1.at[d - 1],
            device_id={"row": 2 * q + core}, device_id_type=MESH)

    def copy5(d):
        q = (chip + d) % 8
        return pltpu.make_async_remote_copy(
            src_ref=unit.at[q], dst_ref=units.at[d - 1], send_sem=s5.at[d - 1], recv_sem=r5.at[d - 1],
            device_id={"row": 2 * q + core}, device_id_type=MESH)

    def copy2(d):
        c = (col + d) % 8
        return pltpu.make_async_remote_copy(
            src_ref=tiles_out.at[c], dst_ref=tiles_in.at[d - 1], send_sem=s2.at[d - 1], recv_sem=r2.at[d - 1],
            device_id={"col": c}, device_id_type=MESH)

    def copy3(d):
        return pltpu.make_async_remote_copy(
            src_ref=mine, dst_ref=every.at[row], send_sem=s3.at[d - 1], recv_sem=r3.at[d - 1],
            device_id={"row": (row + d) % 16}, device_id_type=MESH)

    def copy4(d, j):
        c = (col + d) % 8
        at = pl.ds(pl.multiple_of(j * width, width), width)
        return pltpu.make_async_remote_copy(
            src_ref=send.at[c, :, at], dst_ref=recv.at[d - 1, :, at],
            send_sem=s4.at[d - 1, j], recv_sem=r4.at[d - 1, j],
            device_id={"col": c}, device_id_type=MESH)

    for q in range(8):
        keep(q).start()
    for k in range(CHUNKS):
        fetch(k).start()
    pl.semaphore_wait(barrier, 22)

    for d in (4, 3, 5, 2, 6, 1, 7, 0):
        copy0((chip + d) % 8).start()
    for q in range(8):
        keep(q).wait()
    for d in (4, 3, 5, 2, 6, 1, 7, 0):
        q = (chip + d) % 8
        copy0(q).wait_recv()
        if d == 0:
            acc[q] = acc[q] + got[q]
            continue
        for p in range(2):
            for u in range(2):
                at = pl.ds(64 * u, 64)
                both = acc[q, p, at, :] + got[q, p, at, :]
                top = jnp.maximum(jnp.max(jnp.abs(both), axis=0, keepdims=True), 1e-30)
                coded[q, p, at, :] = jnp.round(both * (32767.0 / top)).astype(jnp.int32).astype(jnp.int16)
                unit[q, pl.ds(2 * p + u, 1), :] = top * (1.0 / 32767.0)
        copy1(d).start()
        copy5(d).start()
    for d in (1, 7, 2, 6, 3, 5, 4):
        copy1(d).wait_recv()
        copy5(d).wait_recv()

    none = jnp.zeros((64, 64), F32)
    wi = jnp.concatenate([none, wi_ref[...]], axis=1)
    wi = jnp.concatenate([wi, wi], axis=0)
    wo = jnp.concatenate([wo_ref[pl.ds(0, 32, 2), :], wo_ref[pl.ds(1, 32, 2), :]], axis=0)
    wo = jnp.concatenate([wo, none], axis=1)
    low = lax.broadcasted_iota(jnp.int32, (64, 128), 1) < 64
    for p in range(2):
        total = acc[chip, p]
        for d in range(7):
            part_of = codes[d, p].astype(jnp.int32).astype(F32)
            total = total + jnp.concatenate([
                part_of[:64] * units[d, pl.ds(2 * p, 1), :], part_of[64:] * units[d, pl.ds(2 * p + 1, 1), :]], axis=0)
        gw = hdot(wo, total, NT)
        hw = hdot(total, wi, NT)
        for u in range(2):
            both = hdot(jnp.where(low if u == 0 else ~low, gw, 0.0), hw, NN)
            rows[pl.ds(2 * p + u, 32, 4), :] = jnp.where(low[:32], both[:32], both[32:])
    tiles_out[...] = rows[...].astype(BF16).reshape(8, 16, 128)
    for d in range(1, 8):
        copy2(d).start()
    tile = tiles_out[col].astype(F32)
    for d in range(1, 8):
        copy2(d).wait_recv()
        tile = tile + tiles_in[d - 1].astype(F32)
    tile = tile.astype(BF16)
    mine[...] = tile
    for d in range(1, 16):
        copy3(d).start()
    every[row] = tile
    for d in range(1, 16):
        copy3(d).wait_recv()

    flat = every[...].reshape(256, 128)
    to = lax.broadcasted_iota(jnp.int32, (64, 256), 0)
    frm = lax.broadcasted_iota(jnp.int32, (64, 256), 1)
    for a in range(4):
        perm = jnp.where(frm == (to // 4) * 16 + 4 * a + to % 4, 1.0, 0.0).astype(BF16)
        query[:, 128 * a:128 * (a + 1)] = lax.dot_general(perm, flat, NN, preferred_element_type=F32).astype(BF16)

    for k in range(CHUNKS):
        fetch(k).wait()

    def score(j, _):
        lo = pl.multiple_of(j * width, width)
        hi = pl.multiple_of(half + j * width, width)
        own = pl.ds(pl.multiple_of(col * 8, 8), 8)
        a = lax.dot_general(query[...], train[pl.ds(lo, width), :], NT, preferred_element_type=F32)
        b = lax.dot_general(query[...], train[pl.ds(hi, width), :], NT, preferred_element_type=F32)
        for c in range(8):
            both = jnp.concatenate([a[8 * c:8 * c + 8], b[8 * c:8 * c + 8]], axis=0)
            send[c, :, pl.ds(lo, width)] = both.astype(BF16)
        for d in (3, 5, 1, 7, 4, 2, 6):
            copy4(d, j).start()
        part[...] = a
        out_ref[:, pl.ds(lo, width)] = part[own, :]
        part[...] = b
        out_ref[:, pl.ds(hi, width)] = part[own, :]
        return 0

    lax.fori_loop(0, CHUNKS, score, 0)

    def collect(j, _):
        lo = pl.ds(pl.multiple_of(j * width, width), width)
        hi = pl.ds(pl.multiple_of(half + j * width, width), width)
        both = jnp.concatenate([out_ref[:, lo], out_ref[:, hi]], axis=0)
        for d in range(1, 8):
            copy4(d, j).wait_recv()
            both = both + recv[d - 1, :, lo].astype(F32)
        out_ref[:, lo] = both[:8]
        out_ref[:, hi] = both[8:]
        return 0

    lax.fori_loop(0, CHUNKS, collect, 0)

    def sent0(q, _):
        copy0(q).wait_send()
        return 0

    lax.fori_loop(0, 8, sent0, 0)
    for d in range(1, 8):
        copy1(d).wait_send()
        copy5(d).wait_send()
        copy2(d).wait_send()
    for d in range(1, 16):
        copy3(d).wait_send()

    def sent4(j, _):
        for d in range(1, 8):
            copy4(d, j).wait_send()
        return 0

    lax.fori_loop(0, CHUNKS, sent4, 0)


def on_device(hidden_acts, out_grads, proj_in, proj_out, white_in, white_out, ep_lengths, flag_ids, train_sketch):
    tokens, width = hidden_acts.shape
    model = out_grads.shape[1]
    n_train, depth = train_sketch.shape
    vmem = pl.BlockSpec(memory_space=pltpu.VMEM)
    smem = pl.BlockSpec(memory_space=pltpu.SMEM)
    dma = pltpu.SemaphoreType.DMA
    hbm = pl.BlockSpec(memory_space=pl.ANY)
    w = pl.pallas_call(
        windows,
        out_shape=jax.ShapeDtypeStruct((32, 128, 128), F32),
        in_specs=[smem, smem, vmem, vmem, hbm, hbm],
        out_specs=vmem,
        scratch_shapes=[
            pltpu.SMEM((64,), jnp.int32),
            pltpu.VMEM((CHUNKS, width, tokens // CHUNKS), BF16),
            pltpu.VMEM((tokens, model), BF16),
            pltpu.VMEM((tokens + 64, 128), F32),
            dma((CHUNKS,)), dma((CHUNKS,)),
        ],
        name="windows",
    )(ep_lengths, flag_ids, proj_in.T, proj_out.T, hidden_acts.T, out_grads)
    return pl.pallas_call(
        kernel,
        out_shape=jax.ShapeDtypeStruct((8, n_train), F32),
        in_specs=[hbm, vmem, vmem, hbm],
        out_specs=vmem,
        scratch_shapes=[
            pltpu.VMEM((n_train, depth), BF16),
            pltpu.VMEM((8, 2, 128, 128), F32),
            pltpu.VMEM((8, 2, 128, 128), F32),
            pltpu.VMEM((8, 2, 128, 128), jnp.int16),
            pltpu.VMEM((8, 4, 128), F32),
            pltpu.VMEM((7, 2, 128, 128), jnp.int16),
            pltpu.VMEM((7, 4, 128), F32),
            pltpu.VMEM((128, 128), F32),
            pltpu.VMEM((8, 16, 128), BF16),
            pltpu.VMEM((7, 16, 128), BF16),
            pltpu.VMEM((16, 128), BF16),
            pltpu.VMEM((16, 16, 128), BF16),
            pltpu.VMEM((64, depth), BF16),
            pltpu.VMEM((64, n_train // 2 // CHUNKS), F32),
            pltpu.VMEM((8, 16, n_train // 2), BF16),
            pltpu.VMEM((7, 16, n_train // 2), BF16),
            dma((CHUNKS,)), dma((8,)),
            dma((8,)), dma((8,)),
            dma((7,)), dma((7,)),
            dma((7,)), dma((7,)),
            dma((7,)), dma((7,)),
            dma((15,)), dma((15,)),
            dma((7, CHUNKS)), dma((7, CHUNKS)),
        ],
        compiler_params=pltpu.CompilerParams(collective_id=0, has_side_effects=True),
        name="attribute",
    )(w, white_in, white_out, train_sketch)


def solution(mesh):
    in_specs = (
        P("col", "row"), P("col", "row"), P("row", None), P("row", None), P(), P(),
        P("col", None), P(), P("row", "col"),
    )
    return jax.shard_map(on_device, mesh=mesh, in_specs=in_specs, out_specs=P("col", "row"), check_vma=False)
```
